32 devices in a mesh: groups: 2 (over x), seq: 16 (over z, y, core).
Axes of the slice: x: 2, y: 2, z: 4, core: 2. Of those that a mesh axis runs over, the one named last changes fastest.
Arguments:
- query_seq: bfloat16 [8192, 6144], P(('groups', 'seq')), parts along dimension 0, may hold values from -15 to 15
- key_seq: bfloat16 [8192, 6144], P(('groups', 'seq')), parts along dimension 0, may hold values from -15 to 15
- value_seq: bfloat16 [8192, 6144], P(('groups', 'seq')), parts along dimension 0, may hold values from -288 to 288
- conv_kernel: bfloat16 [3, 4, 6144], replicated, may hold values from -3 to 3
- feature_map: bfloat16 [128, 128], replicated, may hold values from -1.5 to 1.5
- norm_gain: float32 [6144], replicated, may hold values from 0.25 to 1.75
Outputs:
- attended: bfloat16 [8192, 6144], P(('groups', 'seq')), parts along dimension 0
The draws below stay inside these ranges and needn't reach their ends.
There are 2 independent parts, one for each index of `groups`. The reference program is written for one: setup_inputs(seed, part) draws one part's arguments, and reference() takes and returns one part's arrays. A program takes and returns all parts, laid end to end along the dimension named above; an argument that names none is the same for every part. Nothing has to cross between parts.
All inputs are finite; a program needn't handle non-finite values.
Results may differ from the reference program's by a relative error of at most 0.012.
The reference program's roundings to bfloat16 on the way count: a program that leaves them out, or rounds other values in their place, can miss the bound.
Values may be sent and summed in bfloat16 or wider, within the bound.
A program may use at most 128 MiB of HBM per device.

```python
import math
import jax
import jax.numpy as jnp
from jax import lax

H = 48
DH = 128
D = 6144
SPAN = 256
KCONV = 4
TOKENS = 4096


def draw_value_seq(key, part):
    key_noise = jax.random.fold_in(key, 11)
    key_column = jax.random.fold_in(key, 12)
    key_row = jax.random.fold_in(key, 14)
    noise = jnp.clip(jax.random.normal(key_noise, (TOKENS, D), jnp.float32), -4.0, 4.0)
    column = jnp.exp(jax.random.uniform(key_column, (1, D), jnp.float32) * math.log(10.0))
    row_scale = jnp.exp(jax.random.uniform(key_row, (TOKENS, 1), jnp.float32) * math.log(4.0))
    base = noise * column * row_scale
    earlier = jnp.concatenate([jnp.zeros((1, D), jnp.float32), base[:-1]], axis=0)
    return (base - 0.8 * earlier).astype(jnp.bfloat16)


def draw_feature_map(key, part):
    key_sign = jax.random.fold_in(key, 21)
    key_off = jax.random.fold_in(key, 22)
    signs = (jax.random.randint(key_sign, (DH,), 0, 2) * 2 - 1).astype(jnp.float32)
    off_diag = jnp.clip(jax.random.normal(key_off, (DH, DH), jnp.float32), -4.0, 4.0) * (0.45 / math.sqrt(DH - 1))
    eye = jnp.eye(DH, dtype=jnp.float32)
    return (eye * (1.5 * signs)[None, :] + (1.0 - eye) * off_diag).astype(jnp.bfloat16)


def steps_of(own_key, shape, split, least, high):
    def one(position, blocks):
        draws = jax.random.uniform(jax.random.fold_in(jax.random.fold_in(own_key, 6), position), (blocks,), jnp.float32, least / len(split), high / len(split))
        return jnp.repeat(jnp.exp(draws), shape[position] // blocks).reshape((-1,) + (1,) * (len(shape) - position - 1))

    gain = one(*split[0])
    for cut in split[1:]:
        gain = gain * one(*cut)
    return gain


def gaussian(own_key, dims, width, most, cuts=(), kind=jnp.bfloat16):
    entries = width * jax.random.normal(own_key, dims, jnp.float32)
    if cuts:
        entries = entries * steps_of(own_key, dims, cuts, -0.22, 0.18)
    return jnp.clip(entries, -most, most).astype(kind)


def setup_inputs(seed: int = 0, part: int = 0) -> dict:
    splits = jax.random.split(jax.random.key(seed), 7)
    own_keys = jax.random.split(jax.random.fold_in(splits[6], part), 7)
    query_seq = gaussian(own_keys[0], (TOKENS, D), 3.0, 15.0, ((0, 16),))
    key_seq = gaussian(own_keys[1], (TOKENS, D), 3.0, 15.0, ((0, 16),))
    value_seq = draw_value_seq(jax.random.fold_in(jax.random.fold_in(splits[6], part), 71), part)
    conv_kernel = gaussian(splits[3], (3, KCONV, D), KCONV ** -0.5, 3.0)
    feature_map = draw_feature_map(jax.random.fold_in(splits[6], 71), part)
    norm_gain = jnp.clip(1.0 + 0.15 * jax.random.normal(splits[5], (D,), jnp.float32), 0.25, 1.75)
    return {"query_seq": query_seq, "key_seq": key_seq, "value_seq": value_seq, "conv_kernel": conv_kernel, "feature_map": feature_map, "norm_gain": norm_gain}


def short_conv(seq_rows, kernel):
    tap_count = kernel.shape[0]
    length = seq_rows.shape[0]
    padded = jnp.concatenate([jnp.zeros((tap_count - 1, seq_rows.shape[1]), seq_rows.dtype), seq_rows], axis=0)
    summed = jnp.zeros(seq_rows.shape, jnp.float32)
    for offset in range(tap_count):
        window = padded[tap_count - 1 - offset:tap_count - 1 - offset + length]
        summed = summed + kernel[offset].astype(jnp.float32) * window.astype(jnp.float32)
    return summed.astype(jnp.bfloat16)

def feature_rows(conv_rows, feature_map):
    head_rows = conv_rows.reshape(conv_rows.shape[0], H, DH).astype(jnp.float32)
    projected = jnp.einsum('thd,de->the', head_rows, feature_map.astype(jnp.float32))
    return (jax.nn.elu(projected) + 1.0).astype(jnp.bfloat16)

def reference(query_seq, key_seq, value_seq, conv_kernel, feature_map, norm_gain):
    query_conv = short_conv(query_seq, conv_kernel[0])
    key_conv = short_conv(key_seq, conv_kernel[1])
    value_conv = short_conv(value_seq, conv_kernel[2])
    block_count = TOKENS // SPAN
    query_feat = feature_rows(query_conv, feature_map).reshape(block_count, SPAN, H, DH)
    key_feat = feature_rows(key_conv, feature_map).reshape(block_count, SPAN, H, DH)
    value_heads = value_conv.reshape(block_count, SPAN, H, DH)
    causal = jnp.arange(SPAN)[:, None] >= jnp.arange(SPAN)[None, :]

    def advance(prefix, blocks):
        query_blk, key_blk, value_blk = blocks
        query_wide = query_blk.astype(jnp.float32)
        key_wide = key_blk.astype(jnp.float32)
        value_wide = value_blk.astype(jnp.float32)
        scores = jnp.einsum('ihd,jhd->hij', query_wide, key_wide)
        weights = lax.optimization_barrier(jnp.where(causal[None], scores, 0.0).astype(jnp.bfloat16))
        mixed_rows = jnp.einsum('hij,jhd->ihd', weights.astype(jnp.float32), value_wide)
        prefix_bf = lax.optimization_barrier(prefix.astype(jnp.bfloat16))
        mixed_rows = mixed_rows + jnp.einsum('ihd,hde->ihe', query_wide, prefix_bf.astype(jnp.float32))
        kv_state = jnp.einsum('jhd,jhe->hde', key_wide, value_wide)
        return (prefix + kv_state, mixed_rows)
    start_state = jnp.zeros((H, DH, DH), jnp.float32)
    _, mixed_all = lax.scan(advance, start_state, (query_feat, key_feat, value_heads))
    mixed_all = mixed_all.reshape(TOKENS, H, DH)
    inverse_rms = lax.rsqrt(lax.optimization_barrier(jnp.mean(mixed_all * mixed_all, axis=-1, keepdims=True)) + 1e-06)
    normed = (mixed_all * inverse_rms).reshape(TOKENS, D) * norm_gain
    return normed.astype(jnp.bfloat16)
```

```python
import functools

import jax
import jax.numpy as jnp
from jax import lax
from jax.experimental import pallas as pl
from jax.experimental.pallas import tpu as pltpu
from jax.sharding import PartitionSpec as P

MESH = pl.DeviceIdType.MESH
F32 = jnp.float32
BF16 = jnp.bfloat16
RIM = 8
ROWS = 64
Z_LAG = 2
Y_LAG = 2
P_LAG = 1
Q_LAG = 3


def short_conv(buf, rim, taps, which, col, width):
    tap_rows = taps[which, :, pl.ds(col, width)].astype(F32)
    tap_count = tap_rows.shape[0]
    length = buf.shape[0]
    above = rim[:, pl.ds(col, width)].astype(F32)
    out = []
    for start in range(0, length, ROWS):
        rows = buf[start : start + ROWS, pl.ds(col, width)].astype(F32)
        padded = jnp.concatenate([above, rows], axis=0)
        total = tap_rows[0:1] * rows
        for offset in range(1, tap_count):
            window = padded[RIM - offset : RIM - offset + ROWS]
            total = total + tap_rows[offset : offset + 1] * window
        out.append(total.astype(BF16))
        above = rows[ROWS - RIM :]
    return jnp.concatenate(out, axis=0)


def features(conv_rows, wide_map):
    projected = jnp.dot(conv_rows, wide_map[...], preferred_element_type=F32)
    return jnp.where(projected > 0, projected + 1.0, jnp.exp(projected)).astype(BF16)


def kernel(
    devices,
    q_hbm,
    k_hbm,
    v_hbm,
    taps,
    feature_map,
    gain,
    out_hbm,
    q_buf,
    k_buf,
    v_buf,
    q_rim,
    k_rim,
    v_rim,
    wide_map,
    q_feat,
    k_feat,
    v_conv,
    mixed,
    out_buf,
    own_state,
    x_out,
    x_in,
    z_out,
    z_in,
    y_out,
    y_in,
    p_out,
    prefix,
    load_sem,
    store_sem,
    rim_sem,
    x_sem,
    z_sem,
    y_sem,
    p_sem,
):
    tokens, width = q_buf.shape
    dim = feature_map.shape[0]
    pair = 2 * dim
    chunk = 2 * pair
    chunks = width // chunk
    me = lax.axis_index("seq")
    core = lax.rem(me, 2)
    y = lax.rem(me // 2, 2)
    z = me // 4
    planes = devices // 4
    partner = me + 1 - 2 * core
    across = me + 2 - 4 * y

    def load(hbm, buf, which, c):
        cols = pl.ds(pl.multiple_of(c * chunk, chunk), chunk)
        return pltpu.make_async_copy(hbm.at[:, cols], buf.at[:, cols], load_sem.at[which, c])

    @pl.loop(0, chunks)
    def _(c):
        load(k_hbm, k_buf, 1, c).start()
        load(v_hbm, v_buf, 2, c).start()

    barrier = pltpu.get_barrier_semaphore()

    def greet(target):
        pl.semaphore_signal(barrier, inc=1, device_id={"seq": target}, device_id_type=MESH)

    greet(partner)
    greet(across)

    @pl.when(me > 0)
    def _():
        greet(me - 1)

    @pl.when(me < devices - 1)
    def _():
        greet(me + 1)

    @pl.when(z > 0)
    def _():
        greet(me - 4)

    @pl.when(z < planes - 1)
    def _():
        greet(me + 4)

    @pl.loop(0, chunks)
    def _(c):
        load(q_hbm, q_buf, 0, c).start()

    wide_map[...] = jnp.zeros_like(wide_map)
    wide_map[:dim, :dim] = feature_map[...]
    wide_map[dim:, dim:] = feature_map[...]

    @pl.when(me == 0)
    def _():
        q_rim[...] = jnp.zeros_like(q_rim)
        k_rim[...] = jnp.zeros_like(k_rim)
        v_rim[...] = jnp.zeros_like(v_rim)

    @pl.when(z == 0)
    def _():
        @pl.loop(0, chunks)
        def _(c):
            z_in[c] = jnp.zeros(z_in.shape[1:], BF16)

    edges = [(me > 0), (me < devices - 1), (z > 0), (z < planes - 1)]
    pl.semaphore_wait(barrier, 2 + sum(e.astype(jnp.int32) for e in edges))

    def rim_copy(hbm, rim, which):
        return pltpu.make_async_remote_copy(
            src_ref=hbm.at[pl.ds(tokens - RIM, RIM)],
            dst_ref=rim,
            send_sem=rim_sem.at[0, which],
            recv_sem=rim_sem.at[1, which],
            device_id={"seq": lax.rem(me + 1, devices)},
            device_id_type=MESH,
        )

    rims = [
        rim_copy(k_hbm, k_rim, 1),
        rim_copy(v_hbm, v_rim, 2),
        rim_copy(q_hbm, q_rim, 0),
    ]

    @pl.when(me < devices - 1)
    def _():
        for copy in rims:
            copy.start()

    @pl.when(me > 0)
    def _():
        for copy in rims[:2]:
            copy.wait_recv()

    def send(src, dst, sem, c, target):
        return pltpu.make_async_remote_copy(
            src_ref=src,
            dst_ref=dst,
            send_sem=sem.at[0, c],
            recv_sem=sem.at[1, c],
            device_id={"seq": target},
            device_id_type=MESH,
        )

    def x_copy(c):
        return send(x_out.at[c], x_in.at[c], x_sem, c, partner)

    def z_copy(c):
        return send(z_out.at[c], z_in.at[c], z_sem, c, lax.rem(me + 4, devices))

    def y_copy(c):
        return send(y_out.at[c], y_in.at[c], y_sem, c, across)

    def p_copy(c):
        return send(p_out.at[c], prefix.at[c, core], p_sem, c, partner)

    def pair_state(col):
        k_rows = short_conv(k_buf, k_rim, taps, 1, col, pair)
        v_rows = short_conv(v_buf, v_rim, taps, 2, col, pair)
        feat = features(k_rows, wide_map)
        k_feat[:, pl.ds(col, pair)] = feat
        v_conv[:, pl.ds(col, pair)] = v_rows
        both = lax.dot_general(feat, v_rows, (((0,), (0,)), ((), ())), preferred_element_type=F32)
        return both[:dim, :dim], both[dim:, dim:]

    def states(c):
        load(k_hbm, k_buf, 1, c).wait()
        load(v_hbm, v_buf, 2, c).wait()
        for mine in (False, True):
            side = core if mine else 1 - core
            col = pl.multiple_of(c * chunk + side * pair, pair)
            first, second = pair_state(col)
            if mine:
                own_state[c, :dim] = first
                own_state[c, dim:] = second
            else:
                x_out[c, :dim] = first.astype(BF16)
                x_out[c, dim:] = second.astype(BF16)
                x_copy(c).start()

    def relay_z(c):
        x_copy(c).wait_recv()

        @pl.when(z > 0)
        def _():
            z_copy(c).wait_recv()

        before = z_in[c].astype(F32)
        chip = own_state[c] + x_in[c].astype(F32)
        z_out[c] = (before + chip).astype(BF16)

        @pl.when(z < planes - 1)
        def _():
            z_copy(c).start()

        y_out[c] = (before + jnp.where(y == 0, chip, 0.0)).astype(BF16)
        y_copy(c).start()

    def relay_y(c):
        y_copy(c).wait_recv()
        earlier = z_in[c].astype(F32) + y_in[c].astype(F32)
        p_out[c] = (earlier + jnp.where(core == 0, own_state[c], 0.0)).astype(BF16)
        p_copy(c).start()
        prefix[c, core] = (earlier + jnp.where(core == 1, x_in[c].astype(F32), 0.0)).astype(BF16)

    def local_mix(c):
        load(q_hbm, q_buf, 0, c).wait()
        row = lax.broadcasted_iota(jnp.int32, (tokens, tokens), 0)
        causal = row >= lax.broadcasted_iota(jnp.int32, (tokens, tokens), 1)
        for side in range(2):
            col = pl.multiple_of(c * chunk + side * pair, pair)
            q_rows = short_conv(q_buf, q_rim, taps, 0, col, pair)
            feat = features(q_rows, wide_map)
            q_feat[:, pl.ds(col, pair)] = feat
            for head in range(2):
                cols = pl.ds(pl.multiple_of(col + head * dim, dim), dim)
                scores = lax.dot_general(
                    feat[:, head * dim : (head + 1) * dim],
                    k_feat[:, cols],
                    (((1,), (1,)), ((), ())),
                    preferred_element_type=F32,
                )
                weights = jnp.where(causal, scores, 0.0).astype(BF16)
                mixed[:, cols] = jnp.dot(weights, v_conv[:, cols], preferred_element_type=F32)

    def store(c):
        cols = pl.ds(pl.multiple_of(c * chunk, chunk), chunk)
        return pltpu.make_async_copy(out_buf.at[:, cols], out_hbm.at[:, cols], store_sem.at[c])

    def finish(c):
        p_copy(c).wait_recv()
        for head in range(4):
            cols = pl.ds(pl.multiple_of(c * chunk + head * dim, dim), dim)
            state = prefix[c, head // 2, (head % 2) * dim : (head % 2 + 1) * dim]
            rows = mixed[:, cols] + jnp.dot(q_feat[:, cols], state, preferred_element_type=F32)
            scale = lax.rsqrt(jnp.mean(rows * rows, axis=-1, keepdims=True) + 1e-06)
            out_buf[:, cols] = (rows * scale * gain[:, cols]).astype(BF16)
        store(c).start()

    z_lag = 1 + Z_LAG * z
    y_lag = z_lag + Y_LAG
    last_lag = jnp.maximum(y_lag + P_LAG, Q_LAG)

    def at(step, lag, work):
        c = step - lag

        @pl.when((c >= 0) & (c < chunks))
        def _():
            work(c)

    @pl.loop(0, chunks + last_lag)
    def _(step):
        at(step, 0, states)
        at(step, z_lag, relay_z)
        at(step, y_lag, relay_y)

        @pl.when((me > 0) & (step == Q_LAG))
        def _():
            rims[2].wait_recv()

        at(step, Q_LAG, local_mix)
        at(step, last_lag, finish)

    @pl.when(me < devices - 1)
    def _():
        for copy in rims:
            copy.wait_send()

    @pl.loop(0, chunks)
    def _(c):
        x_copy(c).wait_send()

        @pl.when(z < planes - 1)
        def _():
            z_copy(c).wait_send()

        y_copy(c).wait_send()
        p_copy(c).wait_send()
        store(c).wait()


def on_device(query_seq, key_seq, value_seq, conv_kernel, feature_map, norm_gain):
    tokens, width = query_seq.shape
    dim = feature_map.shape[0]
    devices = lax.axis_size("seq")
    chunks = width // (4 * dim)
    rows = pltpu.VMEM((tokens, width), BF16)
    rim = pltpu.VMEM((RIM, width), BF16)
    slots = pltpu.VMEM((chunks, 2 * dim, dim), BF16)
    ways = pltpu.SemaphoreType.DMA((2, chunks))
    hbm = pl.BlockSpec(memory_space=pl.ANY)
    vmem = pl.BlockSpec(memory_space=pltpu.VMEM)
    return pl.pallas_call(
        functools.partial(kernel, devices),
        out_shape=jax.ShapeDtypeStruct((tokens, width), BF16),
        in_specs=[hbm, hbm, hbm, vmem, vmem, vmem],
        out_specs=hbm,
        scratch_shapes=[
            rows,
            rows,
            rows,
            rim,
            rim,
            rim,
            pltpu.VMEM((2 * dim, 2 * dim), BF16),
            rows,
            rows,
            rows,
            pltpu.VMEM((tokens, width), F32),
            rows,
            pltpu.VMEM((chunks, 2 * dim, dim), F32),
            slots,
            slots,
            slots,
            slots,
            slots,
            slots,
            slots,
            pltpu.VMEM((chunks, 2, 2 * dim, dim), BF16),
            pltpu.SemaphoreType.DMA((3, chunks)),
            pltpu.SemaphoreType.DMA((chunks,)),
            pltpu.SemaphoreType.DMA((2, 3)),
            ways,
            ways,
            ways,
            ways,
        ],
        compiler_params=pltpu.CompilerParams(
            collective_id=0, has_side_effects=True, vmem_limit_bytes=60 * 1024 * 1024
        ),
        name="layer",
    )(query_seq, key_seq, value_seq, conv_kernel, feature_map, norm_gain.reshape(1, width))


def solution(mesh):
    split = P(("groups", "seq"), None)
    return jax.shard_map(
        on_device,
        mesh=mesh,
        in_specs=(split, split, split, P(), P(), P()),
        out_specs=split,
        check_vma=False,
    )
```

```python
import functools

import jax
import jax.numpy as jnp
from jax import lax
from jax.experimental import pallas as pl
from jax.experimental.pallas import tpu as pltpu
from jax.sharding import PartitionSpec as P

MESH = pl.DeviceIdType.MESH
F32 = jnp.float32
BF16 = jnp.bfloat16
RIM = 8
ROWS = 64
Z_LAG = 2
Y_LAG = 3
P_LAG = 2
Q_FIRST = 12
Q_SLOPE = 3


def short_conv(buf, rim, taps, which, col, width):
    tap_rows = taps[which, :, pl.ds(col, width)].astype(F32)
    tap_count = tap_rows.shape[0]
    length = buf.shape[0]
    above = rim[:, pl.ds(col, width)].astype(F32)
    out = []
    for start in range(0, length, ROWS):
        rows = buf[start : start + ROWS, pl.ds(col, width)].astype(F32)
        padded = jnp.concatenate([above, rows], axis=0)
        total = tap_rows[0:1] * rows
        for offset in range(1, tap_count):
            window = padded[RIM - offset : RIM - offset + ROWS]
            total = total + tap_rows[offset : offset + 1] * window
        out.append(total.astype(BF16))
        above = rows[ROWS - RIM :]
    return jnp.concatenate(out, axis=0)


def features(conv_rows, wide_map):
    projected = jnp.dot(conv_rows, wide_map[...], preferred_element_type=F32)
    return jnp.where(projected > 0, projected + 1.0, jnp.exp(projected)).astype(BF16)


def kernel(
    devices,
    q_hbm,
    k_hbm,
    v_hbm,
    taps,
    feature_map,
    gain,
    out_buf,
    q_buf,
    k_buf,
    v_buf,
    q_rim,
    k_rim,
    v_rim,
    wide_map,
    q_feat,
    k_feat,
    v_conv,
    mixed,
    own_state,
    x_out,
    x_in,
    z_out,
    z_in,
    y_out,
    y_in,
    p_out,
    prefix,
    load_sem,
    rim_sem,
    x_sem,
    z_sem,
    y_sem,
    p_sem,
):
    tokens, width = q_buf.shape
    dim = feature_map.shape[0]
    pair = 2 * dim
    chunk = 2 * pair
    chunks = width // chunk
    me = lax.axis_index("seq")
    core = lax.rem(me, 2)
    y = lax.rem(me // 2, 2)
    z = me // 4
    planes = devices // 4
    partner = me + 1 - 2 * core
    across = me + 2 - 4 * y

    def load(hbm, buf, which, c):
        cols = pl.ds(pl.multiple_of(c * chunk, chunk), chunk)
        return pltpu.make_async_copy(hbm.at[:, cols], buf.at[:, cols], load_sem.at[which, c])

    @pl.loop(0, chunks)
    def _(c):
        load(k_hbm, k_buf, 1, c).start()
        load(v_hbm, v_buf, 2, c).start()

    barrier = pltpu.get_barrier_semaphore()

    def greet(target):
        pl.semaphore_signal(barrier, inc=1, device_id={"seq": target}, device_id_type=MESH)

    greet(partner)
    greet(across)

    @pl.when(me > 0)
    def _():
        greet(me - 1)

    @pl.when(me < devices - 1)
    def _():
        greet(me + 1)

    @pl.when(z > 0)
    def _():
        greet(me - 4)

    @pl.when(z < planes - 1)
    def _():
        greet(me + 4)

    @pl.loop(0, chunks)
    def _(c):
        load(q_hbm, q_buf, 0, c).start()

    wide_map[...] = jnp.zeros_like(wide_map)
    wide_map[:dim, :dim] = feature_map[...]
    wide_map[dim:, dim:] = feature_map[...]

    @pl.when(me == 0)
    def _():
        q_rim[...] = jnp.zeros_like(q_rim)
        k_rim[...] = jnp.zeros_like(k_rim)
        v_rim[...] = jnp.zeros_like(v_rim)

    @pl.when(z == 0)
    def _():
        @pl.loop(0, chunks)
        def _(c):
            z_in[c] = jnp.zeros(z_in.shape[1:], BF16)

    edges = [(me > 0), (me < devices - 1), (z > 0), (z < planes - 1)]
    pl.semaphore_wait(barrier, 2 + sum(e.astype(jnp.int32) for e in edges))

    def rim_copy(which, c):
        hbm, rim = ((q_hbm, q_rim), (k_hbm, k_rim), (v_hbm, v_rim))[which]
        cols = pl.ds(pl.multiple_of(c * chunk, chunk), chunk)
        return pltpu.make_async_remote_copy(
            src_ref=hbm.at[pl.ds(tokens - RIM, RIM), cols],
            dst_ref=rim.at[:, cols],
            send_sem=rim_sem.at[0, which, c],
            recv_sem=rim_sem.at[1, which, c],
            device_id={"seq": lax.rem(me + 1, devices)},
            device_id_type=MESH,
        )

    @pl.when(me < devices - 1)
    def _():
        @pl.loop(0, chunks)
        def _(c):
            rim_copy(1, c).start()
            rim_copy(2, c).start()

        @pl.loop(0, chunks)
        def _(c):
            rim_copy(0, c).start()

    def send(src, dst, sem, c, h, target):
        rows = pl.ds(h * dim, dim)
        return pltpu.make_async_remote_copy(
            src_ref=src.at[rows],
            dst_ref=dst.at[rows],
            send_sem=sem.at[0, c, h],
            recv_sem=sem.at[1, c, h],
            device_id={"seq": target},
            device_id_type=MESH,
        )

    def x_copy(c, h):
        return send(x_out.at[c], x_in.at[c], x_sem, c, h, partner)

    def z_copy(c, h):
        return send(z_out.at[c], z_in.at[c], z_sem, c, h, lax.rem(me + 4, devices))

    def y_copy(c, h):
        return send(y_out.at[c], y_in.at[c], y_sem, c, h, across)

    def p_copy(c, h):
        return send(p_out.at[c], prefix.at[c, core], p_sem, c, h, partner)

    def pair_state(col):
        k_rows = short_conv(k_buf, k_rim, taps, 1, col, pair)
        v_rows = short_conv(v_buf, v_rim, taps, 2, col, pair)
        feat = features(k_rows, wide_map)
        k_feat[:, pl.ds(col, pair)] = feat
        v_conv[:, pl.ds(col, pair)] = v_rows
        both = lax.dot_general(feat, v_rows, (((0,), (0,)), ((), ())), preferred_element_type=F32)
        return both[:dim, :dim], both[dim:, dim:]

    def states(c):
        load(k_hbm, k_buf, 1, c).wait()
        load(v_hbm, v_buf, 2, c).wait()

        @pl.when(me > 0)
        def _():
            rim_copy(1, c).wait_recv()
            rim_copy(2, c).wait_recv()

        for mine in (False, True):
            side = core if mine else 1 - core
            col = pl.multiple_of(c * chunk + side * pair, pair)
            first, second = pair_state(col)
            if mine:
                own_state[c, :dim] = first
                own_state[c, dim:] = second
            else:
                x_out[c, :dim] = first.astype(BF16)
                x_out[c, dim:] = second.astype(BF16)

        x_copy(c, 0).start()
        x_copy(c, 1).start()

    def relay_z(c):
        for h in range(2):
            rows = pl.ds(h * dim, dim)
            x_copy(c, h).wait_recv()

            @pl.when(z > 0)
            def _():
                z_copy(c, h).wait_recv()

            before = z_in[c, rows].astype(F32)
            chip = own_state[c, rows] + x_in[c, rows].astype(F32)
            z_out[c, rows] = (before + chip).astype(BF16)

            @pl.when(z < planes - 1)
            def _():
                z_copy(c, h).start()

            y_out[c, rows] = (before + jnp.where(y == 0, chip, 0.0)).astype(BF16)
            y_copy(c, h).start()

    def relay_y(c):
        for h in range(2):
            rows = pl.ds(h * dim, dim)
            y_copy(c, h).wait_recv()
            earlier = z_in[c, rows].astype(F32) + y_in[c, rows].astype(F32)
            p_out[c, rows] = (earlier + jnp.where(core == 0, own_state[c, rows], 0.0)).astype(BF16)
            p_copy(c, h).start()
            own = earlier + jnp.where(core == 1, x_in[c, rows].astype(F32), 0.0)
            prefix[c, core, rows] = own.astype(BF16)

    def local_mix(c):
        load(q_hbm, q_buf, 0, c).wait()

        @pl.when(me > 0)
        def _():
            rim_copy(0, c).wait_recv()

        row = lax.broadcasted_iota(jnp.int32, (tokens, tokens), 0)
        causal = row >= lax.broadcasted_iota(jnp.int32, (tokens, tokens), 1)
        for side in range(2):
            col = pl.multiple_of(c * chunk + side * pair, pair)
            q_rows = short_conv(q_buf, q_rim, taps, 0, col, pair)
            feat = features(q_rows, wide_map)
            q_feat[:, pl.ds(col, pair)] = feat
            for head in range(2):
                cols = pl.ds(pl.multiple_of(col + head * dim, dim), dim)
                scores = lax.dot_general(
                    feat[:, head * dim : (head + 1) * dim],
                    k_feat[:, cols],
                    (((1,), (1,)), ((), ())),
                    preferred_element_type=F32,
                )
                weights = jnp.where(causal, scores, 0.0).astype(BF16)
                mixed[:, cols] = jnp.dot(weights, v_conv[:, cols], preferred_element_type=F32)

    def finish(c):
        p_copy(c, 0).wait_recv()
        p_copy(c, 1).wait_recv()
        for head in range(4):
            cols = pl.ds(pl.multiple_of(c * chunk + head * dim, dim), dim)
            state = prefix[c, head // 2, (head % 2) * dim : (head % 2 + 1) * dim]
            rows = mixed[:, cols] + jnp.dot(q_feat[:, cols], state, preferred_element_type=F32)
            scale = lax.rsqrt(jnp.mean(rows * rows, axis=-1, keepdims=True) + 1e-06)
            out_buf[:, cols] = (rows * scale * gain[:, cols]).astype(BF16)

    z_lag = 1 + Z_LAG * z
    y_lag = z_lag + Y_LAG
    q_lag = jnp.maximum(Q_FIRST - Q_SLOPE * z, 1)
    last_lag = jnp.maximum(y_lag + P_LAG, q_lag)

    def at(step, lag, work):
        c = step - lag

        @pl.when((c >= 0) & (c < chunks))
        def _():
            work(c)

    @pl.loop(0, chunks + last_lag)
    def _(step):
        at(step, 0, states)
        at(step, z_lag, relay_z)
        at(step, y_lag, relay_y)

        at(step, q_lag, local_mix)
        at(step, last_lag, finish)

    @pl.when(me < devices - 1)
    def _():
        @pl.loop(0, chunks)
        def _(c):
            for which in range(3):
                rim_copy(which, c).wait_send()

    @pl.loop(0, chunks)
    def _(c):
        for h in range(2):
            x_copy(c, h).wait_send()
            y_copy(c, h).wait_send()
            p_copy(c, h).wait_send()

    @pl.when(z < planes - 1)
    def _():
        @pl.loop(0, chunks)
        def _(c):
            for h in range(2):
                z_copy(c, h).wait_send()


def on_device(query_seq, key_seq, value_seq, conv_kernel, feature_map, norm_gain):
    tokens, width = query_seq.shape
    dim = feature_map.shape[0]
    devices = lax.axis_size("seq")
    chunks = width // (4 * dim)
    rows = pltpu.VMEM((tokens, width), BF16)
    rim = pltpu.VMEM((RIM, width), BF16)
    slots = pltpu.VMEM((chunks, 2 * dim, dim), BF16)
    ways = pltpu.SemaphoreType.DMA((2, chunks, 2))
    hbm = pl.BlockSpec(memory_space=pl.ANY)
    vmem = pl.BlockSpec(memory_space=pltpu.VMEM)
    return pl.pallas_call(
        functools.partial(kernel, devices),
        out_shape=pltpu.MemorySpace.VMEM((tokens, width), BF16),
        in_specs=[hbm, hbm, hbm, vmem, vmem, vmem],
        out_specs=vmem,
        scratch_shapes=[
            rows,
            rows,
            rows,
            rim,
            rim,
            rim,
            pltpu.VMEM((2 * dim, 2 * dim), BF16),
            rows,
            rows,
            rows,
            pltpu.VMEM((tokens, width), F32),
            pltpu.VMEM((chunks, 2 * dim, dim), F32),
            slots,
            slots,
            slots,
            slots,
            slots,
            slots,
            slots,
            pltpu.VMEM((chunks, 2, 2 * dim, dim), BF16),
            pltpu.SemaphoreType.DMA((3, chunks)),
            pltpu.SemaphoreType.DMA((2, 3, chunks)),
            ways,
            ways,
            ways,
            ways,
        ],
        compiler_params=pltpu.CompilerParams(
            collective_id=0, has_side_effects=True, vmem_limit_bytes=60 * 1024 * 1024
        ),
        name="layer",
    )(query_seq, key_seq, value_seq, conv_kernel, feature_map, norm_gain.reshape(1, width))


def solution(mesh):
    split = P(("groups", "seq"), None)
    return jax.shard_map(
        on_device,
        mesh=mesh,
        in_specs=(split, split, split, P(), P(), P()),
        out_specs=split,
        check_vma=False,
    )
```

```python
import functools

import jax
import jax.numpy as jnp
from jax import lax
from jax.experimental import pallas as pl
from jax.experimental.pallas import tpu as pltpu
from jax.sharding import PartitionSpec as P

MESH = pl.DeviceIdType.MESH
F32 = jnp.float32
BF16 = jnp.bfloat16
RIM = 8
ROWS = 64
Z_LAG = 2
Y_LAG = 3
P_LAG = 2
Q_FIRST = 12
Q_SLOPE = 3


def short_conv(buf, rim, taps, which, col, width):
    tap_rows = taps[which, :, pl.ds(col, width)].astype(F32)
    tap_count = tap_rows.shape[0]
    length = buf.shape[0]
    above = rim[:, pl.ds(col, width)].astype(F32)
    out = []
    for start in range(0, length, ROWS):
        rows = buf[start : start + ROWS, pl.ds(col, width)].astype(F32)
        padded = jnp.concatenate([above, rows], axis=0)
        total = tap_rows[0:1] * rows
        for offset in range(1, tap_count):
            window = padded[RIM - offset : RIM - offset + ROWS]
            total = total + tap_rows[offset : offset + 1] * window
        out.append(total.astype(BF16))
        above = rows[ROWS - RIM :]
    return jnp.concatenate(out, axis=0)


def features(conv_rows, wide_map):
    projected = jnp.dot(conv_rows, wide_map[...], preferred_element_type=F32)
    return jnp.where(projected > 0, projected + 1.0, jnp.exp(projected)).astype(BF16)


def kernel(
    devices,
    q_hbm,
    k_hbm,
    v_hbm,
    taps,
    feature_map,
    gain,
    out_buf,
    q_buf,
    k_buf,
    v_buf,
    q_rim,
    k_rim,
    v_rim,
    wide_map,
    q_feat,
    k_feat,
    v_conv,
    mixed,
    own_state,
    x_out,
    x_in,
    z_out,
    z_in,
    y_out,
    y_in,
    p_out,
    prefix,
    load_sem,
    rim_sem,
    x_sem,
    z_sem,
    y_sem,
    p_sem,
):
    tokens, width = q_buf.shape
    dim = feature_map.shape[0]
    pair = 2 * dim
    chunk = 2 * pair
    chunks = width // chunk
    me = lax.axis_index("seq")
    core = lax.rem(me, 2)
    y = lax.rem(me // 2, 2)
    z = me // 4
    planes = devices // 4
    partner = me + 1 - 2 * core
    across = me + 2 - 4 * y

    def load(hbm, buf, which, c):
        cols = pl.ds(pl.multiple_of(c * chunk, chunk), chunk)
        return pltpu.make_async_copy(hbm.at[:, cols], buf.at[:, cols], load_sem.at[which, c])

    @pl.loop(0, chunks)
    def _(c):
        load(k_hbm, k_buf, 1, c).start()
        load(v_hbm, v_buf, 2, c).start()

    barrier = pltpu.get_barrier_semaphore()

    def greet(target):
        pl.semaphore_signal(barrier, inc=1, device_id={"seq": target}, device_id_type=MESH)

    greet(partner)
    greet(across)

    @pl.when(me > 0)
    def _():
        greet(me - 1)

    @pl.when(me < devices - 1)
    def _():
        greet(me + 1)

    @pl.when(z > 0)
    def _():
        greet(me - 4)

    @pl.when(z < planes - 1)
    def _():
        greet(me + 4)

    @pl.loop(0, chunks)
    def _(c):
        load(q_hbm, q_buf, 0, c).start()

    wide_map[...] = jnp.zeros_like(wide_map)
    wide_map[:dim, :dim] = feature_map[...]
    wide_map[dim:, dim:] = feature_map[...]

    @pl.when(me == 0)
    def _():
        q_rim[...] = jnp.zeros_like(q_rim)
        k_rim[...] = jnp.zeros_like(k_rim)
        v_rim[...] = jnp.zeros_like(v_rim)

    @pl.when(z == 0)
    def _():
        @pl.loop(0, chunks)
        def _(c):
            z_in[c] = jnp.zeros(z_in.shape[1:], BF16)

    edges = [(me > 0), (me < devices - 1), (z > 0), (z < planes - 1)]
    pl.semaphore_wait(barrier, 2 + sum(e.astype(jnp.int32) for e in edges))

    def rim_copy(which, c):
        hbm, rim = ((q_hbm, q_rim), (k_hbm, k_rim), (v_hbm, v_rim))[which]
        cols = pl.ds(pl.multiple_of(c * chunk, chunk), chunk)
        return pltpu.make_async_remote_copy(
            src_ref=hbm.at[pl.ds(tokens - RIM, RIM), cols],
            dst_ref=rim.at[:, cols],
            send_sem=rim_sem.at[0, which, c],
            recv_sem=rim_sem.at[1, which, c],
            device_id={"seq": lax.rem(me + 1, devices)},
            device_id_type=MESH,
        )

    @pl.when(me < devices - 1)
    def _():
        @pl.loop(0, chunks)
        def _(c):
            rim_copy(1, c).start()
            rim_copy(2, c).start()

        @pl.loop(0, chunks)
        def _(c):
            rim_copy(0, c).start()

    def send(src, dst, sem, c, h, target):
        rows = pl.ds(h * dim, dim)
        return pltpu.make_async_remote_copy(
            src_ref=src.at[rows],
            dst_ref=dst.at[rows],
            send_sem=sem.at[0, c, h],
            recv_sem=sem.at[1, c, h],
            device_id={"seq": target},
            device_id_type=MESH,
        )

    def x_copy(c, h):
        return send(x_out.at[c], x_in.at[c], x_sem, c, h, partner)

    def z_copy(c, h):
        return send(z_out.at[c], z_in.at[c], z_sem, c, h, lax.rem(me + 4, devices))

    def y_copy(c, h):
        return send(y_out.at[c], y_in.at[c], y_sem, c, h, across)

    def p_copy(c, h):
        return send(p_out.at[c], prefix.at[c, core], p_sem, c, h, partner)

    def pair_state(col):
        k_rows = short_conv(k_buf, k_rim, taps, 1, col, pair)
        v_rows = short_conv(v_buf, v_rim, taps, 2, col, pair)
        feat = features(k_rows, wide_map)
        k_feat[:, pl.ds(col, pair)] = feat
        v_conv[:, pl.ds(col, pair)] = v_rows
        both = lax.dot_general(feat, v_rows, (((0,), (0,)), ((), ())), preferred_element_type=F32)
        return both[:dim, :dim], both[dim:, dim:]

    def states(c):
        load(k_hbm, k_buf, 1, c).wait()
        load(v_hbm, v_buf, 2, c).wait()

        @pl.when(me > 0)
        def _():
            rim_copy(1, c).wait_recv()
            rim_copy(2, c).wait_recv()

        for mine in (False, True):
            side = core if mine else 1 - core
            col = pl.multiple_of(c * chunk + side * pair, pair)
            first, second = pair_state(col)
            if mine:
                own_state[c, :dim] = first
                own_state[c, dim:] = second
            else:
                x_out[c, :dim] = first.astype(BF16)
                x_out[c, dim:] = second.astype(BF16)

        x_copy(c, 0).start()
        x_copy(c, 1).start()

    def relay_z(c):
        for h in range(2):
            rows = pl.ds(h * dim, dim)
            x_copy(c, h).wait_recv()

            @pl.when(z > 0)
            def _():
                z_copy(c, h).wait_recv()

            before = z_in[c, rows].astype(F32)
            chip = own_state[c, rows] + x_in[c, rows].astype(F32)
            z_out[c, rows] = (before + chip).astype(BF16)

            @pl.when(z < planes - 1)
            def _():
                z_copy(c, h).start()

            y_out[c, rows] = (before + jnp.where(y == 0, chip, 0.0)).astype(BF16)
            y_copy(c, h).start()

    def relay_y(c):
        for h in range(2):
            rows = pl.ds(h * dim, dim)
            y_copy(c, h).wait_recv()
            earlier = z_in[c, rows].astype(F32) + y_in[c, rows].astype(F32)
            p_out[c, rows] = (earlier + jnp.where(core == 0, own_state[c, rows], 0.0)).astype(BF16)
            p_copy(c, h).start()
            own = earlier + jnp.where(core == 1, x_in[c, rows].astype(F32), 0.0)
            prefix[c, core, rows] = own.astype(BF16)

    def local_mix(c):
        load(q_hbm, q_buf, 0, c).wait()

        @pl.when(me > 0)
        def _():
            rim_copy(0, c).wait_recv()

        row = lax.broadcasted_iota(jnp.int32, (tokens, tokens), 0)
        causal = row >= lax.broadcasted_iota(jnp.int32, (tokens, tokens), 1)
        for side in range(2):
            col = pl.multiple_of(c * chunk + side * pair, pair)
            q_rows = short_conv(q_buf, q_rim, taps, 0, col, pair)
            feat = features(q_rows, wide_map)
            q_feat[:, pl.ds(col, pair)] = feat
            for head in range(2):
                cols = pl.ds(pl.multiple_of(col + head * dim, dim), dim)
                scores = lax.dot_general(
                    feat[:, head * dim : (head + 1) * dim],
                    k_feat[:, cols],
                    (((1,), (1,)), ((), ())),
                    preferred_element_type=F32,
                )
                weights = jnp.where(causal, scores, 0.0).astype(BF16)
                mixed[:, cols] = jnp.dot(weights, v_conv[:, cols], preferred_element_type=F32)

    def finish(c):
        p_copy(c, 0).wait_recv()
        p_copy(c, 1).wait_recv()
        for head in range(4):
            cols = pl.ds(pl.multiple_of(c * chunk + head * dim, dim), dim)
            state = prefix[c, head // 2, (head % 2) * dim : (head % 2 + 1) * dim]
            rows = mixed[:, cols] + jnp.dot(q_feat[:, cols], state, preferred_element_type=F32)
            scale = lax.rsqrt(jnp.mean(rows * rows, axis=-1, keepdims=True) + 1e-06)
            out_buf[:, cols] = (rows * scale * gain[:, cols]).astype(BF16)

    z_lag = 1 + Z_LAG * z
    y_lag = z_lag + Y_LAG
    q_lag = jnp.maximum(Q_FIRST - Q_SLOPE * z, 1)
    last_lag = jnp.maximum(y_lag + P_LAG, q_lag)

    def at(step, lag, work):
        c = step - lag

        @pl.when((c >= 0) & (c < chunks))
        def _():
            work(c)

    @pl.loop(0, chunks + last_lag)
    def _(step):
        at(step, 0, states)
        at(step, z_lag, relay_z)
        at(step, q_lag, local_mix)
        at(step, y_lag, relay_y)
        at(step, last_lag, finish)

    @pl.when(me < devices - 1)
    def _():
        @pl.loop(0, chunks)
        def _(c):
            for which in range(3):
                rim_copy(which, c).wait_send()

    @pl.loop(0, chunks)
    def _(c):
        for h in range(2):
            x_copy(c, h).wait_send()
            y_copy(c, h).wait_send()
            p_copy(c, h).wait_send()

    @pl.when(z < planes - 1)
    def _():
        @pl.loop(0, chunks)
        def _(c):
            for h in range(2):
                z_copy(c, h).wait_send()


def on_device(query_seq, key_seq, value_seq, conv_kernel, feature_map, norm_gain):
    tokens, width = query_seq.shape
    dim = feature_map.shape[0]
    devices = lax.axis_size("seq")
    chunks = width // (4 * dim)
    rows = pltpu.VMEM((tokens, width), BF16)
    rim = pltpu.VMEM((RIM, width), BF16)
    slots = pltpu.VMEM((chunks, 2 * dim, dim), BF16)
    ways = pltpu.SemaphoreType.DMA((2, chunks, 2))
    hbm = pl.BlockSpec(memory_space=pl.ANY)
    vmem = pl.BlockSpec(memory_space=pltpu.VMEM)
    return pl.pallas_call(
        functools.partial(kernel, devices),
        out_shape=pltpu.MemorySpace.VMEM((tokens, width), BF16),
        in_specs=[hbm, hbm, hbm, vmem, vmem, vmem],
        out_specs=vmem,
        scratch_shapes=[
            rows,
            rows,
            rows,
            rim,
            rim,
            rim,
            pltpu.VMEM((2 * dim, 2 * dim), BF16),
            rows,
            rows,
            rows,
            pltpu.VMEM((tokens, width), F32),
            pltpu.VMEM((chunks, 2 * dim, dim), F32),
            slots,
            slots,
            slots,
            slots,
            slots,
            slots,
            slots,
            pltpu.VMEM((chunks, 2, 2 * dim, dim), BF16),
            pltpu.SemaphoreType.DMA((3, chunks)),
            pltpu.SemaphoreType.DMA((2, 3, chunks)),
            ways,
            ways,
            ways,
            ways,
        ],
        compiler_params=pltpu.CompilerParams(
            collective_id=0, has_side_effects=True, vmem_limit_bytes=60 * 1024 * 1024
        ),
        name="layer",
    )(query_seq, key_seq, value_seq, conv_kernel, feature_map, norm_gain.reshape(1, width))


def solution(mesh):
    split = P(("groups", "seq"), None)
    return jax.shard_map(
        on_device,
        mesh=mesh,
        in_specs=(split, split, split, P(), P(), P()),
        out_specs=split,
        check_vma=False,
    )
```
